32 devices in a mesh: dp: 8 (over y, x, core), tensor: 4 (over z).
Axes of the slice: x: 2, y: 2, z: 4, core: 2. Of those that a mesh axis runs over, the one named last changes fastest.
Arguments:
- layer_input: bfloat16 [512, 16, 2048], P('tensor', 'dp'), may hold values from -6 to 6
- segments: int32 [16, 512], P('dp'), may hold values from 0 to 2, never falling along the last dimension, each value on 1 to 256 neighbouring positions
- w_query: bfloat16 [1, 2048, 2048], P(None, 'dp', 'tensor'), may hold values from -3 to 3
- w_key: bfloat16 [1, 2048, 2048], P(None, 'dp', 'tensor'), may hold values from -3 to 3
- w_value: bfloat16 [1, 2048, 2048], P(None, 'dp', 'tensor'), may hold values from -0.125 to 0.125
- w_out: bfloat16 [1, 2048, 2048], P(None, 'tensor', 'dp'), may hold values from -0.5 to 0.5
- w_gate: bfloat16 [1, 2048, 8192], P(None, 'dp', 'tensor'), may hold values from -0.125 to 0.125
- w_up: bfloat16 [1, 2048, 8192], P(None, 'dp', 'tensor'), may hold values from -0.125 to 0.125
- w_down: bfloat16 [1, 8192, 2048], P(None, 'tensor', 'dp'), may hold values from -0.0625 to 0.0625
- norm_attn: bfloat16 [1, 2048], P(None, 'dp'), may hold values from 0.5 to 1.5
- norm_mlp: bfloat16 [1, 2048], P(None, 'dp'), may hold values from 0.5 to 1.5
- cotangent: bfloat16 [512, 16, 2048], P('tensor', 'dp'), may hold values from -6 to 6
Outputs:
- layer_output: bfloat16 [512, 16, 2048], P('tensor', 'dp')
- d_x: bfloat16 [512, 16, 2048], P('tensor', 'dp')
- g_query: float32 [1, 2048, 2048], P(None, 'dp', 'tensor')
- g_key: float32 [1, 2048, 2048], P(None, 'dp', 'tensor')
- g_value: float32 [1, 2048, 2048], P(None, 'dp', 'tensor')
- g_out: float32 [1, 2048, 2048], P(None, 'tensor', 'dp')
- g_gate: float32 [1, 2048, 8192], P(None, 'dp', 'tensor')
- g_up: float32 [1, 2048, 8192], P(None, 'dp', 'tensor')
- g_down: float32 [1, 8192, 2048], P(None, 'tensor', 'dp')
- g_norm_attn: float32 [1, 2048], P(None, 'dp')
- g_norm_mlp: float32 [1, 2048], P(None, 'dp')
The draws below stay inside these ranges and needn't reach their ends.
Inputs may be any that keep to these rules, and one draw needn't show every extreme that they name: `segments`: numbers never fall along a sequence; one document holds 1 to 256 positions.
All inputs are finite; a program needn't handle non-finite values.
Results may differ from the reference program's by a relative error of at most 0.018.
Values may be sent and summed in bfloat16 or wider, within the bound.
No kernel may reach another device: no remote copies, remote signals or barrier semaphores. Data moves between devices by JAX's collectives and lax.ppermute only.
A program may use at most 256 MiB of HBM per device.

```python
import math
import jax
import jax.numpy as jnp
import numpy as np
from jax import lax

D = 2048
HEADS = 32
HEAD_DIM = 64
FF = 8192
LAYERS = 1
SEQ = 512
SEQS = 16


def query_key_pair(key):
    base = jax.random.fold_in(key, 17)
    spread = D ** (-0.5)
    noise = jax.random.normal(jax.random.fold_in(base, 2), (LAYERS, D, D), jnp.float32) * spread
    query_draw = jax.random.normal(jax.random.fold_in(base, 1), (LAYERS, D, D), jnp.float32) * spread
    key_draw = noise
    return (jnp.clip(query_draw, -3.0, 3.0), jnp.clip(key_draw, -3.0, 3.0))


def draw_w_query(key, part):
    return query_key_pair(key)[0].astype(jnp.bfloat16)


def draw_w_key(key, part):
    return query_key_pair(key)[1].astype(jnp.bfloat16)


def levels(key, dims, shards, low, high):
    def one(position, blocks):
        draws = jax.random.uniform(jax.random.fold_in(jax.random.fold_in(key, 6), position), (blocks,), jnp.float32, low / len(shards), high / len(shards))
        return jnp.repeat(jnp.exp(draws), dims[position] // blocks).reshape((-1,) + (1,) * (len(dims) - position - 1))

    loudness = one(*shards[0])
    for cut in shards[1:]:
        loudness = loudness * one(*cut)
    return loudness


def profile(amount, total, bound, slope):
    loads = [(1 << 20) // math.isqrt(rank ** slope) + 1 for rank in range(2, amount + 1)]
    spare, holding = total - bound - (amount - 1), [1] * (amount - 1)
    while spare > 0:
        movable = [i for i in range(amount - 1) if holding[i] < bound]
        mass, remaining = sum([loads[i] for i in movable]), spare
        for i in movable:
            extra = min(bound - holding[i], max(1, remaining * loads[i] // mass), spare)
            holding[i] = holding[i] + extra
            spare = spare - extra
    return np.array([bound] + holding)


def ragged(key, number_of, total, most, skew):
    if number_of == 2:
        one = jax.random.randint(key, (), max(1, total - most), min(most, total - 1) + 1)
        return jnp.stack([one, total - one])
    lengths = jnp.asarray(profile(number_of, total, most, skew), jnp.int32)
    twos = (number_of - 1) // 2
    donor, sink = lengths[1:1 + 2 * twos:2], lengths[2:2 + 2 * twos:2]
    room = jnp.minimum(donor - 1, most - sink)
    shifted = jax.random.randint(jax.random.fold_in(key, 1), (twos,), 0, 1 << 20) % (room + 1)
    lengths = lengths.at[1:1 + 2 * twos:2].set(donor - shifted).at[2:2 + 2 * twos:2].set(sink + shifted)
    return lengths[jax.random.permutation(jax.random.fold_in(key, 2), number_of)]


def centred(stream_key, extent, scale, bound, pieces=(), kind=jnp.bfloat16):
    result = jax.random.normal(stream_key, extent, jnp.float32) * scale
    if len(pieces) > 0:
        result = levels(stream_key, extent, pieces, -0.22, 0.18) * result
    return jnp.clip(result, min=-bound, max=bound).astype(kind)


def setup_inputs(seed: int = 0) -> dict:
    seeds = jax.random.split(jax.random.key(seed), 13)
    layer_input = centred(seeds[0], (SEQ, SEQS, D), 1.0, 6.0, ((0, 4), (1, 8)))
    segments = jax.vmap(lambda own: jnp.searchsorted(jnp.cumsum(ragged(own, 3, SEQ, SEQ // 2, 0)), jnp.arange(SEQ), side="right"))(jax.random.split(seeds[1], SEQS)).reshape((SEQS, SEQ)).astype(jnp.int32)
    w_query = draw_w_query(jax.random.fold_in(seeds[12], 71), 0)
    w_key = draw_w_key(jax.random.fold_in(seeds[12], 71), 0)
    w_value = centred(seeds[4], (LAYERS, D, D), D ** -0.5, 0.125, ((1, 8), (2, 4)))
    w_out = centred(seeds[5], (LAYERS, D, D), (D // 16) ** -0.5, 0.5, ((1, 4), (2, 8)))
    w_gate = centred(seeds[6], (LAYERS, D, FF), D ** -0.5, 0.125, ((1, 8), (2, 4)))
    w_up = centred(seeds[7], (LAYERS, D, FF), D ** -0.5, 0.125, ((1, 8), (2, 4)))
    w_down = centred(seeds[8], (LAYERS, FF, D), FF ** -0.5, 0.0625, ((1, 4), (2, 8)))
    norm_attn = jnp.clip(1.0 + 0.1 * jax.random.normal(seeds[9], (LAYERS, D), jnp.float32), 0.5, 1.5).astype(jnp.bfloat16)
    norm_mlp = jnp.clip(1.0 + 0.1 * jax.random.normal(seeds[10], (LAYERS, D), jnp.float32), 0.5, 1.5).astype(jnp.bfloat16)
    cotangent = centred(seeds[11], (SEQ, SEQS, D), 1.0, 6.0, ((0, 4), (1, 8)))
    return dict(layer_input=layer_input, segments=segments, w_query=w_query, w_key=w_key, w_value=w_value, w_out=w_out, w_gate=w_gate, w_up=w_up, w_down=w_down, norm_attn=norm_attn, norm_mlp=norm_mlp, cotangent=cotangent)


EPSILON = 1e-05
THETA = 130000.0
NEGATIVE = -1e+30

def rope_tables(length, head_width):
    half_width = head_width // 2
    freqs = THETA ** (-(jnp.arange(half_width, dtype=jnp.float32) * 2.0) / head_width)
    angles = jnp.arange(length, dtype=jnp.float32)[:, None] * freqs[None, :]
    angles = jnp.concatenate([angles, angles], axis=1)
    return (jnp.cos(angles), jnp.sin(angles))

def rotate(tensor, cosines, sines):
    half_width = tensor.shape[-1] // 2
    swapped = jnp.concatenate([-tensor[..., half_width:], tensor[..., :half_width]], axis=-1)
    return tensor * cosines + swapped * sines

def rotate_back(grad_in, cosines, sines):
    half_width = grad_in.shape[-1] // 2
    scaled = grad_in * sines
    swapped = jnp.concatenate([scaled[..., half_width:], -scaled[..., :half_width]], axis=-1)
    return grad_in * cosines + swapped

def normalize(stream, gain_vec):
    inv_rms = lax.rsqrt(lax.optimization_barrier(jnp.mean(stream * stream, axis=-1, keepdims=True)) + EPSILON)
    return ((stream * inv_rms * gain_vec.astype(jnp.float32)).astype(jnp.bfloat16), inv_rms)

def norm_backward(stream, inv_rms, gain_vec, grad_normed):
    scaled = gain_vec.astype(jnp.float32) * grad_normed
    grad_stream = inv_rms * scaled - stream * (inv_rms * inv_rms * inv_rms) * lax.optimization_barrier(jnp.mean(scaled * stream, axis=-1, keepdims=True))
    grad_gain = lax.optimization_barrier(jnp.sum((grad_normed * stream * inv_rms).reshape(-1, stream.shape[-1]), axis=0))
    return (grad_stream, grad_gain)

def attend(queries, key_rows, value_rows, allowed, scale):
    scores = jnp.einsum('qhd,khd->hqk', queries.astype(jnp.float32), key_rows.astype(jnp.float32)) * scale
    scores = jnp.where(allowed[None], scores, NEGATIVE)
    row_max = lax.optimization_barrier(jnp.max(scores, axis=-1, keepdims=True))
    log_total = row_max + jnp.log(lax.optimization_barrier(jnp.sum(jnp.exp(scores - row_max), axis=-1, keepdims=True)))
    softmax_p = jnp.exp(scores - log_total).astype(jnp.bfloat16)
    attended = jnp.einsum('hqk,khd->qhd', softmax_p.astype(jnp.float32), value_rows.astype(jnp.float32)).astype(jnp.bfloat16)
    return (attended, log_total)

def attend_back(queries, key_rows, value_rows, allowed, scale, log_total, grad_att):
    scores = jnp.einsum('qhd,khd->hqk', queries.astype(jnp.float32), key_rows.astype(jnp.float32)) * scale
    scores = jnp.where(allowed[None], scores, NEGATIVE)
    probs_f = jnp.exp(scores - log_total)
    softmax_p = probs_f.astype(jnp.bfloat16)
    grad_p = jnp.einsum('qhd,khd->hqk', grad_att.astype(jnp.float32), value_rows.astype(jnp.float32))
    row_delta = lax.optimization_barrier(jnp.sum(probs_f * grad_p, axis=-1, keepdims=True))
    grad_scores = (probs_f * (grad_p - row_delta)).astype(jnp.bfloat16)
    grad_q = jnp.einsum('hqk,khd->qhd', grad_scores.astype(jnp.float32), key_rows.astype(jnp.float32)) * scale
    grad_k = jnp.einsum('hqk,qhd->khd', grad_scores.astype(jnp.float32), queries.astype(jnp.float32)) * scale
    grad_v = jnp.einsum('hqk,qhd->khd', softmax_p.astype(jnp.float32), grad_att.astype(jnp.float32)).astype(jnp.bfloat16)
    return (grad_q, grad_k, grad_v)

def layer_forward(stream, weights, allowed, cosines, sines, scale):
    query_w, key_w, value_w, out_w, gate_w, up_w, down_w, gain_a, gain_m = weights
    length = stream.shape[0]
    shape_heads = (length, HEADS, HEAD_DIM)
    normed_a, inv_rms_a = normalize(stream, gain_a)
    queries = rotate(jnp.dot(normed_a, query_w, preferred_element_type=jnp.float32).reshape(shape_heads), cosines, sines).astype(jnp.bfloat16)
    key_rows = rotate(jnp.dot(normed_a, key_w, preferred_element_type=jnp.float32).reshape(shape_heads), cosines, sines).astype(jnp.bfloat16)
    value_rows = jnp.dot(normed_a, value_w, preferred_element_type=jnp.float32).astype(jnp.bfloat16).reshape(shape_heads)
    attended, log_total = attend(queries, key_rows, value_rows, allowed, scale)
    attended_flat = attended.reshape(length, HEADS * HEAD_DIM)
    middle = stream + jnp.dot(attended_flat, out_w, preferred_element_type=jnp.float32)
    normed_m, inv_rms_m = normalize(middle, gain_m)
    gate_pre = jnp.dot(normed_m, gate_w, preferred_element_type=jnp.float32)
    up_proj = jnp.dot(normed_m, up_w, preferred_element_type=jnp.float32)
    hidden = (jax.nn.silu(gate_pre) * up_proj).astype(jnp.bfloat16)
    after = middle + jnp.dot(hidden, down_w, preferred_element_type=jnp.float32)
    stored = (stream, inv_rms_a, normed_a, queries, key_rows, value_rows, attended_flat, log_total, middle, inv_rms_m, normed_m, gate_pre, up_proj, hidden)
    return (after, stored)

def layer_backward(grad, stored, weights, allowed, cosines, sines, scale):
    query_w, key_w, value_w, out_w, gate_w, up_w, down_w, gain_a, gain_m = weights
    stream, inv_rms_a, normed_a, queries, key_rows, value_rows, attended_flat, log_total, middle, inv_rms_m, normed_m, gate_pre, up_proj, hidden = stored
    length = stream.shape[0]
    branch_m = grad.astype(jnp.bfloat16)
    grad_down_w = jnp.dot(hidden.T, branch_m, preferred_element_type=jnp.float32)
    grad_hidden = jnp.dot(branch_m, down_w.T, preferred_element_type=jnp.float32)
    sigmoid_g = jax.nn.sigmoid(gate_pre)
    grad_up_b = (grad_hidden * gate_pre * sigmoid_g).astype(jnp.bfloat16)
    grad_gate_b = (grad_hidden * up_proj * sigmoid_g * (1.0 + gate_pre * (1.0 - sigmoid_g))).astype(jnp.bfloat16)
    grad_gate_w = jnp.dot(normed_m.T, grad_gate_b, preferred_element_type=jnp.float32)
    grad_up_w = jnp.dot(normed_m.T, grad_up_b, preferred_element_type=jnp.float32)
    grad_normed_m = jnp.dot(grad_gate_b, gate_w.T, preferred_element_type=jnp.float32) + jnp.dot(grad_up_b, up_w.T, preferred_element_type=jnp.float32)
    grad_mid, gain_part_m = norm_backward(middle, inv_rms_m, gain_m, grad_normed_m)
    grad_mid = grad_mid + grad
    branch_a = grad_mid.astype(jnp.bfloat16)
    grad_out_w = jnp.dot(attended_flat.T, branch_a, preferred_element_type=jnp.float32)
    grad_att = jnp.dot(branch_a, out_w.T, preferred_element_type=jnp.float32).astype(jnp.bfloat16).reshape(length, HEADS, HEAD_DIM)
    grad_q, grad_k, grad_v = attend_back(queries, key_rows, value_rows, allowed, scale, log_total, grad_att)
    grad_q = rotate_back(grad_q, cosines, sines).astype(jnp.bfloat16).reshape(length, -1)
    grad_k = rotate_back(grad_k, cosines, sines).astype(jnp.bfloat16).reshape(length, -1)
    grad_v = grad_v.reshape(length, -1)
    grad_query_w = jnp.dot(normed_a.T, grad_q, preferred_element_type=jnp.float32)
    grad_key_w = jnp.dot(normed_a.T, grad_k, preferred_element_type=jnp.float32)
    grad_value_w = jnp.dot(normed_a.T, grad_v, preferred_element_type=jnp.float32)
    grad_normed_a = jnp.dot(grad_q, query_w.T, preferred_element_type=jnp.float32) + jnp.dot(grad_k, key_w.T, preferred_element_type=jnp.float32) + jnp.dot(grad_v, value_w.T, preferred_element_type=jnp.float32)
    grad_in, gain_part_a = norm_backward(stream, inv_rms_a, gain_a, grad_normed_a)
    grad_in = grad_in + grad_mid
    return (grad_in, (grad_query_w, grad_key_w, grad_value_w, grad_out_w, grad_gate_w, grad_up_w, grad_down_w, gain_part_a, gain_part_m))

def reference(layer_input, segments, w_query, w_key, w_value, w_out, w_gate, w_up, w_down, norm_attn, norm_mlp, cotangent):
    scale = 1.0 / math.sqrt(HEAD_DIM)
    cosines, sines = rope_tables(SEQ, HEAD_DIM)
    cosines = cosines[:, None, :]
    sines = sines[:, None, :]
    positions = jnp.arange(SEQ, dtype=jnp.int32)
    params = (w_query, w_key, w_value, w_out, w_gate, w_up, w_down, norm_attn, norm_mlp)

    def one_sequence(totals, inputs):
        tokens, segment_row, cot_row = inputs
        allowed = (segment_row[:, None] == segment_row[None, :]) & (positions[None, :] <= positions[:, None])
        stream = tokens.astype(jnp.float32)
        stored_all = []
        for layer_id in range(LAYERS):
            weights = tuple((member[layer_id] for member in params))
            stream, stored = layer_forward(stream, weights, allowed, cosines, sines, scale)
            stored_all.append(stored)
        output = stream.astype(jnp.bfloat16)
        grad = cot_row.astype(jnp.float32)
        for layer_id in reversed(range(LAYERS)):
            weights = tuple((member[layer_id] for member in params))
            grad, grads_here = layer_backward(grad, stored_all[layer_id], weights, allowed, cosines, sines, scale)
            totals = tuple((summed.at[layer_id].add(portion) for summed, portion in zip(totals, grads_here)))
        return (totals, (output, grad.astype(jnp.bfloat16)))
    zeros = tuple((jnp.zeros(member.shape, jnp.float32) for member in params))
    totals, (outputs, grads_x) = lax.scan(one_sequence, zeros, (jnp.swapaxes(layer_input, 0, 1), segments, jnp.swapaxes(cotangent, 0, 1)))
    return (jnp.swapaxes(outputs, 0, 1), jnp.swapaxes(grads_x, 0, 1), totals[0], totals[1], totals[2], totals[3], totals[4], totals[5], totals[6], totals[7], totals[8])
```

```python
import math

import jax
import jax.numpy as jnp
import numpy as np
from jax import lax
from jax.experimental import pallas as pl
from jax.experimental.pallas import tpu as pltpu
from jax.sharding import PartitionSpec as P

HEAD_DIM = 64
EPSILON = 1e-05
THETA = 130000.0
NEGATIVE = -1e30


def rope_tables(length, head_width):
    half_width = head_width // 2
    freqs = THETA ** (-(jnp.arange(half_width, dtype=jnp.float32) * 2.0) / head_width)
    angles = jnp.arange(length, dtype=jnp.float32)[:, None] * freqs[None, :]
    angles = jnp.concatenate([angles, angles], axis=1)
    return (jnp.cos(angles), jnp.sin(angles))


def rotate(tensor, cosines, sines):
    half_width = tensor.shape[-1] // 2
    swapped = jnp.concatenate([-tensor[..., half_width:], tensor[..., :half_width]], axis=-1)
    return tensor * cosines + swapped * sines


def rotate_back(grad_in, cosines, sines):
    half_width = grad_in.shape[-1] // 2
    scaled = grad_in * sines
    swapped = jnp.concatenate([scaled[..., half_width:], -scaled[..., :half_width]], axis=-1)
    return grad_in * cosines + swapped


def normalize(stream, gain):
    inv_rms = lax.rsqrt(jnp.mean(stream * stream, axis=-1, keepdims=True) + EPSILON)
    return ((stream * inv_rms * gain).astype(jnp.bfloat16), inv_rms)


def norm_backward(stream, inv_rms, gain, grad_normed):
    scaled = gain * grad_normed
    grad_stream = inv_rms * scaled - stream * (inv_rms * inv_rms * inv_rms) * jnp.mean(
        scaled * stream, axis=-1, keepdims=True
    )
    grad_gain = jnp.sum(grad_normed * stream * inv_rms, axis=0)
    return (grad_stream, grad_gain)


def attend(queries, key_rows, value_rows, allowed, scale):
    scores = jnp.einsum("qhd,khd->hqk", queries, key_rows, preferred_element_type=jnp.float32)
    scores = jnp.where(allowed[None], scores * scale, NEGATIVE)
    row_max = jnp.max(scores, axis=-1, keepdims=True)
    log_total = row_max + jnp.log(jnp.sum(jnp.exp(scores - row_max), axis=-1, keepdims=True))
    softmax_p = jnp.exp(scores - log_total).astype(jnp.bfloat16)
    attended = jnp.einsum(
        "hqk,khd->qhd", softmax_p, value_rows, preferred_element_type=jnp.float32
    ).astype(jnp.bfloat16)
    return (attended, log_total)


def attend_back(queries, key_rows, value_rows, allowed, scale, log_total, grad_att):
    scores = jnp.einsum("qhd,khd->hqk", queries, key_rows, preferred_element_type=jnp.float32)
    scores = jnp.where(allowed[None], scores * scale, NEGATIVE)
    probs_f = jnp.exp(scores - log_total)
    softmax_p = probs_f.astype(jnp.bfloat16)
    grad_p = jnp.einsum("qhd,khd->hqk", grad_att, value_rows, preferred_element_type=jnp.float32)
    row_delta = jnp.sum(probs_f * grad_p, axis=-1, keepdims=True)
    grad_scores = (probs_f * (grad_p - row_delta)).astype(jnp.bfloat16)
    grad_q = (
        jnp.einsum("hqk,khd->qhd", grad_scores, key_rows, preferred_element_type=jnp.float32)
        * scale
    )
    grad_k = (
        jnp.einsum("hqk,qhd->khd", grad_scores, queries, preferred_element_type=jnp.float32)
        * scale
    )
    grad_v = jnp.einsum(
        "hqk,qhd->khd", softmax_p, grad_att, preferred_element_type=jnp.float32
    ).astype(jnp.bfloat16)
    return (grad_q, grad_k, grad_v)


def dot(left, right):
    return jnp.dot(left, right, preferred_element_type=jnp.float32)


def dot_t(left, right):
    return lax.dot_general(left, right, (((1,), (1,)), ((), ())), preferred_element_type=jnp.float32)


def t_dot(left, right):
    return lax.dot_general(left, right, (((0,), (0,)), ((), ())), preferred_element_type=jnp.float32)


class Hyper:
    def __init__(self, size):
        self.size = size
        bits = size.bit_length() - 1
        chip_bits = list(range(1, bits))
        self.orders = (chip_bits, chip_bits[::-1])
        self.entries = []
        for core in range(2):
            for path, order in enumerate(self.orders):
                for index in range(1 << len(order)):
                    offset = core
                    for place, bit in enumerate(order):
                        offset |= ((index >> place) & 1) << bit
                    self.entries.append((offset, path))

    def swap(self, value, bit):
        return lax.ppermute(value, "dp", [(i, i ^ (1 << bit)) for i in range(self.size)])

    def gather_half(self, shard):
        rows = shard.shape[0] // 2
        done = []
        for path, order in enumerate(self.orders):
            held = shard[path * rows : (path + 1) * rows]
            for bit in order:
                held = jnp.concatenate([held, self.swap(held, bit)], axis=0)
            done.append(held)
        return jnp.concatenate(done, axis=0)

    def gather(self, shard):
        half = self.gather_half(shard)
        return jnp.concatenate([half, self.swap(half, 0)], axis=0)

    def scatter(self, own_half, other_half):
        kind = own_half.dtype
        held = own_half.astype(jnp.float32) + self.swap(other_half, 0).astype(jnp.float32)
        rows = held.shape[0] // 2
        done = []
        for path, order in enumerate(self.orders):
            part = held[path * rows : (path + 1) * rows]
            for bit in order[::-1]:
                middle = part.shape[0] // 2
                sent = part[middle:].astype(kind)
                part = part[:middle] + self.swap(sent, bit).astype(jnp.float32)
            done.append(part)
        return jnp.concatenate(done, axis=0)

    def sources(self, index, blocks):
        return jnp.stack([(index ^ offset) * 2 + path for offset, path in self.entries])

    def targets(self, index):
        place = {entry: j for j, entry in enumerate(self.entries)}
        table = jnp.array(
            [[place[(o, path)] for path in range(2)] for o in range(self.size)], jnp.int32
        )
        owners = jnp.arange(self.size, dtype=jnp.int32) ^ index
        return table[owners].reshape(-1)


class Line:
    def __init__(self, size):
        self.size = size

    def move(self, value, pairs):
        return lax.ppermute(value, "tensor", pairs)

    def slots(self, index):
        if self.size == 4:
            table = jnp.array(
                [[0, 1, 2, 3], [1, 0, 2, 3], [2, 3, 1, 0], [3, 2, 1, 0]], jnp.int32
            )
            return table[index]
        return (index + jnp.arange(self.size, dtype=jnp.int32)) % self.size

    def gather(self, own):
        n = self.size
        if n == 4:
            outer, inner = [(0, 1), (1, 0), (2, 3), (3, 2)], [(1, 2), (2, 1)]
            ends = [(1, 0), (2, 3)]
            first = self.move(own, outer)
            across = self.move(own, inner)
            far = self.move(first, inner)
            to_end = self.move(across, ends)
            far_end = self.move(far, ends)
            return [own, first, across + to_end, far + far_end]
        ups, downs = [own], [own]
        for k in range(1, n):
            ups.append(self.move(ups[-1], [(i, i + 1) for i in range(k - 1, n - 1)]))
            downs.append(self.move(downs[-1], [(i + 1, i) for i in range(0, n - k)]))
        return [own] + [downs[r] + ups[n - r] for r in range(1, n)]

    def scatter(self, parts):
        n = self.size
        f32 = jnp.float32
        kind = parts[0].dtype

        def add(one, *others):
            total = one.astype(f32)
            for other in others:
                total = total + other.astype(f32)
            return total

        if n == 4:
            outer, inner = [(0, 1), (1, 0), (2, 3), (3, 2)], [(1, 2), (2, 1)]
            ends = [(0, 1), (3, 2)]
            far = add(parts[3], self.move(parts[3], ends)).astype(kind)
            across = add(parts[2], self.move(parts[2], ends)).astype(kind)
            first = add(parts[1], self.move(far, inner)).astype(kind)
            return add(parts[0], self.move(across, inner), self.move(first, outer))
        up, down = parts[n - 1], parts[1]
        for k in range(1, n):
            up_in = self.move(up, [(i, i + 1) for i in range(0, k)])
            down_in = self.move(down, [(i, i - 1) for i in range(n - k, n)])
            if k < n - 1:
                up = add(parts[n - 1 - k], up_in).astype(kind)
                down = add(parts[k + 1], down_in).astype(kind)
        return add(parts[0], up_in, down_in)

    def total(self, value):
        step = 1
        while step < self.size:
            value = value + self.move(value, [(i, i ^ step) for i in range(self.size)])
            step *= 2
        return value


def move_blocks(source, order):
    rows, width = source.shape
    count = order.shape[0]
    block = width // count
    if block % 128:
        return source.reshape(rows, count, block)[:, order, :].reshape(rows, width)

    def kernel(order_ref, in_ref, out_ref):
        for j in range(count):
            start = pl.multiple_of(order_ref[j] * block, block)
            out_ref[:, j * block : (j + 1) * block] = in_ref[:, pl.ds(start, block)]

    return pl.pallas_call(
        kernel,
        grid_spec=pltpu.PrefetchScalarGridSpec(
            num_scalar_prefetch=1,
            grid=(1,),
            in_specs=[pl.BlockSpec((rows, width), lambda i, order: (0, 0))],
            out_specs=pl.BlockSpec((rows, width), lambda i, order: (0, 0)),
        ),
        out_shape=jax.ShapeDtypeStruct((rows, width), source.dtype),
    )(order, source)


def build(mesh):
    hyper = Hyper(mesh.shape["dp"])
    line = Line(mesh.shape["tensor"])
    n = mesh.shape["tensor"]

    def per_device(
        layer_input, segments, w_query, w_key, w_value, w_out, w_gate, w_up, w_down,
        norm_attn, norm_mlp, cotangent,
    ):
        rows, seqs, width = layer_input.shape
        seq_len = segments.shape[1]
        scale = 1.0 / math.sqrt(HEAD_DIM)
        here, place = lax.axis_index("dp"), lax.axis_index("tensor")
        sources = hyper.sources(here, None)
        targets = hyper.targets(here)
        slots = line.slots(place)
        positions = (slots[:, None] * rows + jnp.arange(rows, dtype=jnp.int32)).reshape(-1)
        cosines, sines = rope_tables(seq_len, HEAD_DIM)
        cosines = cosines.reshape(n, rows, HEAD_DIM)[slots].reshape(seq_len, 1, HEAD_DIM)
        sines = sines.reshape(n, rows, HEAD_DIM)[slots].reshape(seq_len, 1, HEAD_DIM)
        seg = segments.reshape(seqs, n, rows)[:, slots, :].reshape(seqs, seq_len)

        blocks = 2 * mesh.shape["dp"]
        gains = jnp.stack([norm_attn.reshape(2, -1), norm_mlp.reshape(2, -1)], axis=1)
        gains = hyper.gather(gains.reshape(2, -1)).reshape(blocks, 2, -1)
        gain_a = gains[:, 0].reshape(1, width).astype(jnp.float32)
        gain_m = gains[:, 1].reshape(1, width).astype(jnp.float32)
        qkv_w = hyper.gather(jnp.concatenate([w_query[0], w_key[0], w_value[0]], axis=1))
        out_t = hyper.gather(w_out[0].T)
        gate_w = hyper.gather(w_gate[0])
        up_w = hyper.gather(w_up[0])
        down_t = hyper.gather(w_down[0].T)
        heads_width = out_t.shape[1]
        heads = heads_width // HEAD_DIM

        def slotted(value):
            return [value[i * rows : (i + 1) * rows] for i in range(n)]

        def spread(value):
            return jnp.concatenate(line.gather(value), axis=0)

        ids = range(seqs)
        x = [move_blocks(layer_input[:, s, :], sources).astype(jnp.float32) for s in ids]
        cot = [move_blocks(cotangent[:, s, :], sources) for s in ids]
        allowed = [
            (seg[s][:, None] == seg[s][None, :]) & (positions[None, :] <= positions[:, None])
            for s in ids
        ]
        shape_heads = (seq_len, heads, HEAD_DIM)
        flat_a, inv_a, att, saved = [], [], [], []
        middle, flat_m, inv_m = [], [], []
        for s in ids:
            normed, inv = normalize(x[s], gain_a)
            flat_a.append(spread(normed))
            inv_a.append(inv)
        flat_c = [spread(cot[s]) for s in ids]
        for s in ids:
            qkv = dot(flat_a[s], qkv_w)
            q, k, v = (
                qkv[:, i * heads_width : (i + 1) * heads_width].reshape(shape_heads)
                for i in range(3)
            )
            q = rotate(q, cosines, sines).astype(jnp.bfloat16)
            k = rotate(k, cosines, sines).astype(jnp.bfloat16)
            v = v.astype(jnp.bfloat16)
            attended, log_total = attend(q, k, v, allowed[s], scale)
            attended = attended.reshape(seq_len, heads_width)
            att.append(attended)
            saved.append((q, k, v, log_total))
            part = dot_t(attended, out_t).astype(jnp.bfloat16)
            mid = x[s] + line.scatter(slotted(part))
            middle.append(mid)
            normed, inv = normalize(mid, gain_m)
            inv_m.append(inv)
            flat_m.append(spread(normed))
        hidden, g_gate, g_up, outs, grad_mid, gain_parts_m, flat_b = [], [], [], [], [], [], []
        for s in ids:
            gate = dot(flat_m[s], gate_w)
            up = dot(flat_m[s], up_w)
            g_hidden = dot(flat_c[s], down_t)
            sig = jax.nn.sigmoid(gate)
            hid = (gate * sig * up).astype(jnp.bfloat16)
            hidden.append(hid)
            g_up.append((g_hidden * gate * sig).astype(jnp.bfloat16))
            g_gate.append((g_hidden * up * sig * (1.0 + gate * (1.0 - sig))).astype(jnp.bfloat16))
            part = (dot_t(g_gate[s], gate_w) + dot_t(g_up[s], up_w)).astype(jnp.bfloat16)
            g_normed = line.scatter(slotted(part))
            grad, gain_part = norm_backward(middle[s], inv_m[s], gain_m, g_normed)
            grad = grad + cot[s].astype(jnp.float32)
            grad_mid.append(grad)
            gain_parts_m.append(gain_part)
            flat_b.append(spread(grad.astype(jnp.bfloat16)))
        for s in ids:
            part = dot_t(hidden[s], down_t).astype(jnp.bfloat16)
            after = middle[s] + line.scatter(slotted(part))
            outs.append(move_blocks(after.astype(jnp.bfloat16), targets))
        d_x, d_qkv, gain_parts_a = [], [], []
        for s in ids:
            q, k, v, log_total = saved[s]
            g_att = dot(flat_b[s], out_t).astype(jnp.bfloat16).reshape(shape_heads)
            g_q, g_k, g_v = attend_back(q, k, v, allowed[s], scale, log_total, g_att)
            g_q = rotate_back(g_q, cosines, sines).astype(jnp.bfloat16)
            g_k = rotate_back(g_k, cosines, sines).astype(jnp.bfloat16)
            d_qkv.append(
                jnp.concatenate([g.reshape(seq_len, heads_width) for g in (g_q, g_k, g_v)], axis=1)
            )
            part = dot_t(d_qkv[s], qkv_w).astype(jnp.bfloat16)
            g_normed = line.scatter(slotted(part))
            grad, gain_part = norm_backward(x[s], inv_a[s], gain_a, g_normed)
            gain_parts_a.append(gain_part)
            d_x.append(move_blocks((grad + grad_mid[s]).astype(jnp.bfloat16), targets))

        def weight_grad(lefts, rights):
            left, right = jnp.concatenate(lefts, axis=0), jnp.concatenate(rights, axis=0)
            half = width // 2
            other = t_dot(left[:, half:], right).astype(jnp.bfloat16)
            own = t_dot(left[:, :half], right).astype(jnp.bfloat16)
            return hyper.scatter(own, other)

        grad_down = weight_grad(flat_c, hidden)
        grad_gate = weight_grad(flat_m, g_gate)
        grad_up = weight_grad(flat_m, g_up)
        grad_out = weight_grad(flat_b, att)
        grad_qkv = weight_grad(flat_a, d_qkv)
        gain_sum = jnp.stack([sum(gain_parts_a), sum(gain_parts_m)]).reshape(2, blocks, -1)
        gain_sum = line.total(gain_sum.transpose(1, 0, 2).reshape(blocks, -1))
        gain_sum = hyper.scatter(gain_sum[: blocks // 2], gain_sum[blocks // 2 :])
        gain_sum = gain_sum.reshape(2, 2, -1).transpose(1, 0, 2).reshape(2, -1)
        return (
            jnp.stack(outs, axis=1),
            jnp.stack(d_x, axis=1),
            grad_qkv[None, :, :heads_width],
            grad_qkv[None, :, heads_width : 2 * heads_width],
            grad_qkv[None, :, 2 * heads_width :],
            grad_out.T[None],
            grad_gate[None],
            grad_up[None],
            grad_down.T[None],
            gain_sum[:1],
            gain_sum[1:],
        )

    return per_device


def solution(mesh):
    placed = (
        P("tensor", "dp", None),
        P("dp", None),
        P(None, "dp", "tensor"),
        P(None, "dp", "tensor"),
        P(None, "dp", "tensor"),
        P(None, "tensor", "dp"),
        P(None, "dp", "tensor"),
        P(None, "dp", "tensor"),
        P(None, "tensor", "dp"),
        P(None, "dp"),
        P(None, "dp"),
        P("tensor", "dp", None),
    )
    return jax.shard_map(
        build(mesh),
        mesh=mesh,
        in_specs=placed,
        out_specs=(
            P("tensor", "dp", None),
            P("tensor", "dp", None),
            P(None, "dp", "tensor"),
            P(None, "dp", "tensor"),
            P(None, "dp", "tensor"),
            P(None, "tensor", "dp"),
            P(None, "dp", "tensor"),
            P(None, "dp", "tensor"),
            P(None, "tensor", "dp"),
            P(None, "dp"),
            P(None, "dp"),
        ),
        check_vma=False,
    )
```

```python
import math

import jax
import jax.numpy as jnp
from jax import lax
from jax.experimental import pallas as pl
from jax.experimental.pallas import tpu as pltpu
from jax.sharding import PartitionSpec as P

HEAD_DIM = 64
EPSILON = 1e-05
THETA = 130000.0
NEGATIVE = -1e30
F32 = jnp.float32
BF16 = jnp.bfloat16


def rope_tables(length, head_width):
    half_width = head_width // 2
    freqs = THETA ** (-(jnp.arange(half_width, dtype=jnp.float32) * 2.0) / head_width)
    angles = jnp.arange(length, dtype=jnp.float32)[:, None] * freqs[None, :]
    angles = jnp.concatenate([angles, angles], axis=1)
    return (jnp.cos(angles), jnp.sin(angles))


def dot(left, right):
    return jnp.dot(left, right, preferred_element_type=F32)


def dot_t(left, right):
    return lax.dot_general(left, right, (((1,), (1,)), ((), ())), preferred_element_type=F32)


def t_dot(left, right):
    return lax.dot_general(left, right, (((0,), (0,)), ((), ())), preferred_element_type=F32)


def fit(size, most):
    while size % most:
        most //= 2
    return most


class Cube:
    def __init__(self, size):
        self.size = size
        self.bits = list(range(1, size.bit_length() - 1))
        self.entries = [core + 2 * i for core in range(2) for i in range(size // 2)]

    def swap(self, value, bit, name):
        with jax.named_scope(name):
            return lax.ppermute(value, "dp", [(i, i ^ (1 << bit)) for i in range(self.size)])

    def gather(self, shard, name):
        if len(self.bits) == 2 and shard.shape[0] % 2 == 0:
            one, two = self.bits
            rows = shard.shape[0] // 2
            first = self.swap(shard, one, name + "_x")
            second = self.swap(shard, two, name + "_y")
            upper = self.swap(first[:rows], two, name + "_xy")
            lower = self.swap(second[rows:], one, name + "_yx")
            held = [shard, first, second, upper, lower]
        else:
            held = [shard]
            for bit in self.bits:
                both = jnp.concatenate(held, axis=0)
                held = held + [self.swap(both, bit, f"{name}_b{bit}")]
        across = [self.swap(piece, 0, f"{name}_c{i}") for i, piece in enumerate(held)]
        return jnp.concatenate(held + across, axis=0)

    def scatter(self, own_half, other_half, name):
        kind = own_half.dtype
        other = self.swap(other_half, 0, name + "_c")
        held = (own_half.astype(F32) + other.astype(F32)).astype(kind)
        groups = [list(range(core, self.size, 2)) for core in range(2)]
        with jax.named_scope(name + "_rs"):
            return lax.psum_scatter(
                held, "dp", scatter_dimension=0, axis_index_groups=groups, tiled=True
            ).astype(F32)

    def sources(self, index):
        return jnp.array(self.entries, jnp.int32) ^ index

    def targets(self, index):
        places = jnp.array([self.entries.index(i) for i in range(self.size)], jnp.int32)
        return places[jnp.arange(self.size, dtype=jnp.int32) ^ index]


class Line:
    def __init__(self, size):
        self.size = size

    def move(self, value, pairs, name):
        with jax.named_scope(name):
            return lax.ppermute(value, "tensor", pairs)

    def slots(self, index):
        if self.size == 4:
            table = jnp.array(
                [[0, 1, 2, 3], [1, 0, 2, 3], [2, 3, 1, 0], [3, 2, 1, 0]], jnp.int32
            )
            return table[index]
        return (index + jnp.arange(self.size, dtype=jnp.int32)) % self.size

    def gather(self, own, name):
        n = self.size
        if n == 4:
            outer, inner = [(0, 1), (1, 0), (2, 3), (3, 2)], [(1, 2), (2, 1)]
            ends = [(1, 0), (2, 3)]
            first = self.move(own, outer, name + "_1")
            across = self.move(own, inner, name + "_2")
            far = self.move(first, inner, name + "_3")
            to_end = self.move(across, ends, name + "_4")
            far_end = self.move(far, ends, name + "_5")
            return [(own,), (first,), (across, to_end), (far, far_end)]
        ups, downs = [own], [own]
        for k in range(1, n):
            up, down = [(i, i + 1) for i in range(k - 1, n - 1)], [(i + 1, i) for i in range(n - k)]
            ups.append(self.move(ups[-1], up, f"{name}_u{k}"))
            downs.append(self.move(downs[-1], down, f"{name}_d{k}"))
        return [(own,)] + [(downs[r], ups[n - r]) for r in range(1, n)]

    def scatter(self, parts, name):
        n = self.size
        kind = parts[0].dtype

        def add(one, other):
            with jax.named_scope(name + "_add"):
                return (one.astype(F32) + other.astype(F32)).astype(kind)

        if n == 4:
            outer, inner = [(0, 1), (1, 0), (2, 3), (3, 2)], [(1, 2), (2, 1)]
            ends = [(0, 1), (3, 2)]
            far = add(parts[3], self.move(parts[3], ends, name + "_1"))
            across = add(parts[2], self.move(parts[2], ends, name + "_2"))
            first = add(parts[1], self.move(far, inner, name + "_3"))
            return (
                parts[0],
                self.move(across, inner, name + "_4"),
                self.move(first, outer, name + "_5"),
            )
        up, down = parts[n - 1], parts[1]
        for k in range(1, n):
            up_in = self.move(up, [(i, i + 1) for i in range(0, k)], f"{name}_u{k}")
            down_in = self.move(down, [(i, i - 1) for i in range(n - k, n)], f"{name}_d{k}")
            if k < n - 1:
                up = add(parts[n - 1 - k], up_in)
                down = add(parts[k + 1], down_in)
        return (parts[0], up_in, down_in)

    def total(self, value, name):
        step = 1
        while step < self.size:
            pairs = [(i, i ^ step) for i in range(self.size)]
            value = value + self.move(value, pairs, f"{name}_{step}")
            step *= 2
        return value


def whole(shape):
    return pl.BlockSpec(shape, lambda *_: (0,) * len(shape))


def shaped(shape, dtype):
    return jax.ShapeDtypeStruct(shape, dtype)


def normed(stream, gain):
    inv = lax.rsqrt(jnp.mean(stream * stream, axis=-1, keepdims=True) + EPSILON)
    return (stream * inv * gain).astype(BF16)


def call(kernel, grid, in_specs, out_specs, out_shape, name, scalars=(), scratch=()):
    with_scalars = pltpu.PrefetchScalarGridSpec(
        num_scalar_prefetch=len(scalars), grid=grid, in_specs=in_specs, out_specs=out_specs,
        scratch_shapes=scratch,
    )

    def run(*args):
        with jax.named_scope(name):
            return pl.pallas_call(
                kernel, grid_spec=with_scalars, out_shape=out_shape, name=name.split("_")[0]
            )(*scalars, *args)

    return run


def enter(source, order, pieces, name):
    seqs, rows, width = source.shape
    count = order.shape[0]
    block = width // count
    each = seqs // pieces

    def kernel(order_ref, in_ref, *refs):
        outs, sem = refs[:-1], refs[-1]
        copies = [
            pltpu.make_async_copy(
                in_ref.at[s, :, pl.ds(pl.multiple_of(order_ref[j] * block, block), block)],
                outs[s // each].at[
                    s % each * rows : (s % each + 1) * rows, j * block : (j + 1) * block
                ],
                sem.at[s * count + j],
            )
            for s in range(seqs)
            for j in range(count)
        ]
        for copy in copies:
            copy.start()
        for copy in copies:
            copy.wait()

    return call(
        kernel, (1,), [pl.BlockSpec(memory_space=pl.ANY)],
        [whole((each * rows, width))] * pieces,
        [shaped((each * rows, width), BF16)] * pieces, name, (order,),
        [pltpu.SemaphoreType.DMA((count * seqs,))],
    )(source)


def leave(values, order, name):
    rows, width = values[0].shape
    count = order.shape[0]
    block = width // count
    seqs = len(values)

    def kernel(order_ref, *refs):
        out_ref, sem = refs[-2:]
        copies = [
            pltpu.make_async_copy(
                ref.at[:, pl.ds(pl.multiple_of(order_ref[j] * block, block), block)],
                out_ref.at[:, s * width + j * block : s * width + (j + 1) * block],
                sem.at[s * count + j],
            )
            for s, ref in enumerate(refs[:-2])
            for j in range(count)
        ]
        for copy in copies:
            copy.start()
        for copy in copies:
            copy.wait()

    out = call(
        kernel, (1,), [pl.BlockSpec(memory_space=pl.ANY)] * seqs,
        whole((rows, width * seqs)), shaped((rows, width * seqs), values[0].dtype), name,
        (order,), [pltpu.SemaphoreType.DMA((count * seqs,))],
    )(*values)
    return out.reshape(rows, seqs, width)


def middle_step(stream, addends, gain, name):
    rows, width = stream.shape

    def kernel(stream_ref, *refs):
        gain_ref, mid_ref, out_ref = refs[-3:]
        mid = stream_ref[...].astype(F32)
        for ref in refs[:-3]:
            mid = mid + ref[...].astype(F32)
        mid_ref[...] = mid
        out_ref[...] = normed(mid, gain_ref[...])

    tile = fit(rows, 64)
    spec = pl.BlockSpec((tile, width), lambda i: (i, 0))
    return call(
        kernel, (rows // tile,), [spec] * (1 + len(addends)) + [whole((1, width))], [spec, spec],
        [shaped((rows, width), F32), shaped((rows, width), BF16)], name,
    )(stream, *addends, gain)


def back_step(stream, addends, gain, grad, name, wide=True):
    rows, width = stream.shape
    count = len(addends)

    def kernel(stream_ref, *refs):
        gain_ref, grad_ref, *outs = refs[count:]
        value = stream_ref[...].astype(F32)
        g_normed = refs[0][...].astype(F32)
        for ref in refs[1:count]:
            g_normed = g_normed + ref[...].astype(F32)
        inv = lax.rsqrt(jnp.mean(value * value, axis=-1, keepdims=True) + EPSILON)
        scaled = gain_ref[...] * g_normed
        inner = jnp.mean(scaled * value, axis=-1, keepdims=True)
        total = grad_ref[...].astype(F32) + (inv * scaled - value * (inv * inv * inv) * inner)
        outs[0][...] = total.astype(BF16)
        if wide:
            outs[1][...] = total

    tile = fit(rows, 64)
    spec = pl.BlockSpec((tile, width), lambda i: (i, 0))
    kinds = [BF16, F32] if wide else [BF16]
    return call(
        kernel, (rows // tile,), [spec] * (1 + count) + [whole((1, width)), spec],
        [spec] * len(kinds), [shaped((rows, width), kind) for kind in kinds], name,
    )(stream, *addends, gain, grad)


def fill(groups, refs, ids_ref, out_ref, rows, change=None):
    at = 0
    for i, size in enumerate(groups):
        value = refs[at][...]
        for k in range(1, size):
            value = value + refs[at + k][...]
        at += size
        if change is not None:
            value = change(value)
        out_ref[pl.ds(pl.multiple_of(ids_ref[i] * rows, rows), rows), :] = value


def project(slots, ids, weight, start, columns, kind, tile, name, gain=None):
    rows, width = slots[0][0].shape
    total = rows * len(slots)
    tile = fit(columns, tile)
    skip = start // tile
    flat = [a for group in slots for a in group]
    groups = [len(group) for group in slots]
    gains = [] if gain is None else [gain]

    def kernel(ids_ref, *refs):
        weight_ref, flat_ref, out_ref = refs[-3:]

        @pl.when(pl.program_id(0) == 0)
        def _():
            change = None
            if gains:
                change = lambda value: normed(value.astype(F32), refs[len(flat)][...])
            fill(groups, refs, ids_ref, flat_ref, rows, change)

        out_ref[...] = dot(flat_ref[...], weight_ref[...]).astype(kind)

    return call(
        kernel, (columns // tile,),
        [whole((rows, width))] * len(flat) + [whole((1, width))] * len(gains)
        + [pl.BlockSpec((width, tile), lambda j, ids: (0, j + skip))],
        [whole((total, width)), pl.BlockSpec((total, tile), lambda j, ids: (0, j))],
        [shaped((total, width), BF16), shaped((total, columns), kind)], name, (ids,),
    )(*flat, *gains, weight)


def expand(slots, slots_c, which, ids, gate_up, down_t, tile, name):
    rows, width = slots[0][0].shape
    total, units = rows * len(slots), down_t.shape[1]
    tile = fit(units, tile)
    flat = [a for group in slots for a in group]
    flat_c = [a for group in slots_c for a in group]
    groups = [len(group) for group in slots]

    def kernel(ids_ref, *refs):
        gate_ref, up_ref, down_ref, m_ref, c_ref, hid_ref, gg_ref, gu_ref = refs[-8:]

        @pl.when(pl.program_id(0) == 0)
        def _():
            fill(groups, refs, ids_ref, m_ref, rows)
            fill(groups, refs[len(flat) :], ids_ref, c_ref, rows)

        gate = dot(m_ref[...], gate_ref[...])
        up = dot(m_ref[...], up_ref[...])
        g_hidden = dot(c_ref[...], down_ref[...])
        sig = jax.nn.sigmoid(gate)
        act = gate * sig
        hid_ref[...] = (act * up).astype(BF16)
        gu_ref[...] = (g_hidden * act).astype(BF16)
        gg_ref[...] = (g_hidden * up * (sig * (1.0 + gate * (1.0 - sig)))).astype(BF16)

    steps = units // tile
    column = pl.BlockSpec((total, tile), lambda j, ids: (0, j))
    return call(
        kernel, (steps,),
        [whole((rows, width))] * len(flat)
        + [pl.BlockSpec((rows, width), lambda j, ids: (which, 0))] * len(flat_c)
        + [
            pl.BlockSpec((width, tile), lambda j, ids: (0, j)),
            pl.BlockSpec((width, tile), lambda j, ids: (0, j + steps)),
            pl.BlockSpec((width, tile), lambda j, ids: (0, j)),
        ],
        [whole((total, width))] * 2 + [column] * 3,
        [shaped((total, width), BF16)] * 2 + [shaped((total, units), BF16)] * 3, name, (ids,),
    )(*flat, *flat_c, gate_up, gate_up, down_t)


def contract(lefts, ids, weight, skip, pieces, tile, name):
    total, width = lefts[0][0].shape[0], weight.shape[0]
    rows = total // pieces
    seqs, count = len(lefts), len(lefts[0])
    tile = fit(width, tile)
    flat = [a for group in lefts for a in group]

    def kernel(ids_ref, *refs):
        weights, outs = refs[seqs * count : (seqs + 1) * count], refs[(seqs + 1) * count :]
        for s in range(seqs):
            acc = None
            for i in range(count):
                ref = refs[s * count + i]
                left = jnp.concatenate(
                    [
                        ref[pl.ds(pl.multiple_of(ids_ref[p] * rows, rows), rows), :]
                        for p in range(pieces)
                    ],
                    axis=0,
                )
                part = dot_t(left, weights[i][...])
                acc = part if acc is None else acc + part
            acc = acc.astype(BF16)
            for p in range(pieces):
                outs[p][s * rows : (s + 1) * rows, :] = acc[p * rows : (p + 1) * rows]

    def columns(i, left):
        return pl.BlockSpec((tile, left.shape[1]), lambda j, ids: (j, i + skip))

    return call(
        kernel, (width // tile,),
        [whole(left.shape) for left in flat]
        + [columns(i, left) for i, left in enumerate(lefts[0])],
        [pl.BlockSpec((seqs * rows, tile), lambda j, ids: (0, j))] * pieces,
        [shaped((seqs * rows, width), BF16)] * pieces, name, (ids,),
    )(*flat, *([weight] * count))


def weight_half(lefts, rights, half, chip, steps, name):
    total, width = lefts[0].shape
    height = width // 2
    tile = height // steps
    sizes = [group[0].shape[1] for group in rights]
    count = len(lefts)
    flat = [a for group in rights for a in group]

    def kernel(chip_ref, *refs):
        out_ref = refs[-1]
        at = 0
        for g, size in enumerate(sizes):
            acc = t_dot(refs[0][...], refs[count + g * count][...])
            for s in range(1, count):
                acc = acc + t_dot(refs[s][...], refs[count + g * count + s][...])
            out_ref[:, at : at + size] = acc.astype(BF16)
            at += size

    return call(
        kernel, (steps,),
        [pl.BlockSpec((total, tile), lambda i, chip: (0, i + half * steps))] * count
        + [whole(a.shape) for a in flat],
        pl.BlockSpec((tile, sum(sizes)), lambda i, chip: (i ^ chip[0], 0)),
        shaped((height, sum(sizes)), BF16), name, (chip,),
    )(*lefts, *flat)


def turn(value, cosines, low, high):
    return (
        value * cosines
        + pltpu.roll(value, value.shape[1] - HEAD_DIM // 2, 1) * low
        + pltpu.roll(value, HEAD_DIM // 2, 1) * high
    )


def spans(total, block, longest):
    for r in range(total // block):
        start = max(0, (r * block - longest + 1) // block * block)
        yield slice(r * block, (r + 1) * block), slice(start, (r + 1) * block)


def attend(qkv, tables, bias, columns, scale, longest, name):
    total = qkv.shape[0]
    lanes = 2 * HEAD_DIM
    steps = columns // lanes
    block = fit(total, 128)

    def kernel(q_in, k_in, v_in, cos_ref, low_ref, high_ref, bias_ref, *outs):
        att_ref, q_ref, k_ref, v_ref, lse_ref = outs
        cosines, low, high = cos_ref[...], low_ref[...], high_ref[...]
        q_ref[...] = (turn(q_in[...], cosines, low, high) * scale).astype(BF16)
        k_ref[...] = turn(k_in[...], cosines, low, high).astype(BF16)
        v_ref[...] = v_in[...].astype(BF16)
        for head in range(2):
            at = slice(head * HEAD_DIM, (head + 1) * HEAD_DIM)
            for here, keys in spans(total, block, longest):
                scores = dot_t(q_ref[here, at], k_ref[keys, at]) + bias_ref[here, keys]
                top = jnp.max(scores, axis=-1, keepdims=True)
                probs = jnp.exp(scores - top)
                size = jnp.sum(probs, axis=-1, keepdims=True)
                mixed = dot(probs.astype(BF16), v_ref[keys, at]) / size
                att_ref[here, at] = mixed.astype(BF16)
                lse_ref[here, at] = jnp.broadcast_to(top + jnp.log(size), (block, HEAD_DIM))

    def part(i):
        return pl.BlockSpec((total, lanes), lambda j: (0, j + i * steps))

    return call(
        kernel, (steps,),
        [part(0), part(1), part(2)] + [whole((total, lanes))] * 3 + [whole((total, total))],
        [part(0)] * 5,
        [shaped((total, columns), BF16)] * 4 + [shaped((total, columns), F32)], name,
    )(qkv, qkv, qkv, *tables, bias)


def attend_back(saved, grad_att, tables, bias, scale, longest, name):
    q, k, v, lse = saved
    total, columns = q.shape
    lanes = 2 * HEAD_DIM
    steps = columns // lanes
    block = fit(total, 128)

    def kernel(q_ref, k_ref, v_ref, lse_ref, g_ref, cos_ref, low_ref, high_ref, bias_ref, *refs):
        dq_out, dk_out, dv_out, dq_ref, dk_ref, dv_ref = refs
        dk_ref[...] = jnp.zeros_like(dk_ref)
        dv_ref[...] = jnp.zeros_like(dv_ref)
        for head in range(2):
            at = slice(head * HEAD_DIM, (head + 1) * HEAD_DIM)
            for here, keys in spans(total, block, longest):
                q_r, g_r, k_r = q_ref[here, at], g_ref[here, at], k_ref[keys, at]
                scores = dot_t(q_r, k_r) + bias_ref[here, keys]
                probs = jnp.exp(scores - lse_ref[here, head * HEAD_DIM : head * HEAD_DIM + 1])
                grad_p = dot_t(g_r, v_ref[keys, at])
                delta = jnp.sum(probs * grad_p, axis=-1, keepdims=True)
                grad_s = (probs * (grad_p - delta)).astype(BF16)
                dq_ref[here, at] = dot(grad_s, k_r)
                dk_ref[keys, at] += t_dot(grad_s, q_r)
                dv_ref[keys, at] += t_dot(probs.astype(BF16), g_r)
        cosines, low, high = cos_ref[...], -low_ref[...], -high_ref[...]
        dq_out[...] = turn(dq_ref[...] * scale, cosines, low, high).astype(BF16)
        dk_out[...] = turn(dk_ref[...], cosines, low, high).astype(BF16)
        dv_out[...] = dv_ref[...].astype(BF16)

    part = pl.BlockSpec((total, lanes), lambda j: (0, j))
    return call(
        kernel, (steps,),
        [part] * 5 + [whole((total, lanes))] * 3 + [whole((total, total))],
        [part] * 3, [shaped((total, columns), BF16)] * 3, name,
        scratch=[pltpu.VMEM((total, lanes), F32)] * 3,
    )(q, k, v, lse, grad_att, *tables, bias)


def build(mesh):
    cube = Cube(mesh.shape["dp"])
    line = Line(mesh.shape["tensor"])
    n = mesh.shape["tensor"]

    def per_device(
        layer_input, segments, w_query, w_key, w_value, w_out, w_gate, w_up, w_down,
        norm_attn, norm_mlp, cotangent,
    ):
        rows, seqs, width = layer_input.shape
        seq_len = segments.shape[1]
        longest = seq_len // 2
        scale = 1.0 / math.sqrt(HEAD_DIM)
        here, place = lax.axis_index("dp"), lax.axis_index("tensor")
        chip = (here // 2).astype(jnp.int32).reshape(1)
        chips = mesh.shape["dp"] // 2
        sources, targets = cube.sources(here), cube.targets(here)
        ids = line.slots(place)
        positions = jnp.arange(seq_len, dtype=jnp.int32)
        cosines, sines = rope_tables(seq_len, HEAD_DIM)
        first = jnp.arange(HEAD_DIM) < HEAD_DIM // 2
        tables = [
            jnp.tile(table, (1, 2))
            for table in (cosines, jnp.where(first, -sines, 0.0), jnp.where(first, 0.0, sines))
        ]
        heads_width = w_query.shape[2]
        units = w_gate.shape[2]
        every = range(seqs)

        gains = jnp.concatenate([norm_attn, norm_mlp], axis=0).T
        gains = jnp.pad(gains, ((0, 0), (0, 128 - gains.shape[1])))
        attn_own = jnp.concatenate([w_query[0], w_key[0], w_value[0], w_out[0].T, gains], axis=1)
        mlp_own = jnp.concatenate([w_gate[0], w_up[0]], axis=1)
        x = enter(layer_input.transpose(1, 0, 2), sources, seqs, "enter_x")
        slots_a = [line.gather(x[s], f"ga{s}") for s in every]
        attn_w = cube.gather(attn_own, "wa")
        (cot,) = enter(cotangent.transpose(1, 0, 2), sources, 1, "enter_c")
        slots_c = line.gather(cot, "gc")
        down_t = cube.gather(w_down[0].T, "wd")
        gate_up = cube.gather(mlp_own, "wm")
        gains = attn_w[:, 4 * heads_width : 4 * heads_width + 2].T.astype(F32)
        gain_a, gain_m = gains[:1], gains[1:]
        bias = [
            jnp.where(
                (segments[s][:, None] == segments[s][None, :])
                & (positions[None, :] <= positions[:, None]),
                0.0, NEGATIVE,
            ).astype(F32)
            for s in every
        ]
        flat_a, att, saved, mid, slots_m = ([] for _ in range(5))
        for s in every:
            flat, qkv = project(
                slots_a[s], ids, attn_w, 0, 3 * heads_width, F32, 512, f"qkv_{s}", gain_a
            )
            flat_a.append(flat)
            attended, *rest = attend(qkv, tables, bias[s], heads_width, scale, longest, f"attend_{s}")
            att.append(attended)
            saved.append(rest)
            parts = contract([[attended]], ids, attn_w, 3, n, 512, f"out_{s}")
            middle, normed_m = middle_step(x[s], line.scatter(parts, f"ro{s}"), gain_m, f"mid_{s}")
            mid.append(middle)
            slots_m.append(line.gather(normed_m, f"gm{s}"))
        flat_m, flat_c, hidden, g_gate, g_up, g_mid, slots_b = ([] for _ in range(7))
        for s in every:
            fm, fc, hid, gg, gu = expand(
                slots_m[s], slots_c, s, ids, gate_up, down_t, 256, f"expand_{s}"
            )
            flat_m.append(fm)
            flat_c.append(fc)
            hidden.append(hid)
            g_gate.append(gg)
            g_up.append(gu)
            parts = contract([[gg, gu]], ids, gate_up, 0, n, 256, f"back_{s}")
            low, grad = back_step(
                mid[s], line.scatter(parts, f"rm{s}"), gain_m, cot[s * rows : (s + 1) * rows],
                f"bmid_{s}",
            )
            g_mid.append(grad)
            slots_b.append(line.gather(low, f"gb{s}"))

        def weight_grad(lefts, rights, name):
            other = weight_half(lefts, rights, 1, chip, chips, name + "_h1")
            own = weight_half(lefts, rights, 0, chip, chips, name + "_h0")
            return cube.scatter(own, other, "s" + name)

        grad_down = weight_grad(flat_c, [hidden], "wgd")
        grad_gu = weight_grad(flat_m, [g_gate, g_up], "wgm")
        parts = contract([[h] for h in hidden], ids, down_t, 0, n, 512, "down")
        addends = line.scatter(parts, "rd")
        outs = []
        for s in every:
            total = mid[s]
            for addend in addends:
                total = total + addend[s * rows : (s + 1) * rows].astype(F32)
            outs.append(total.astype(BF16))
        d_x, flat_b, d_qkv = [], [], []
        for s in every:
            fb, g_att = project(
                slots_b[s], ids, attn_w, 3 * heads_width, heads_width, BF16, 512, f"gatt_{s}"
            )
            flat_b.append(fb)
            grads = attend_back(saved[s], g_att, tables, bias[s], scale, longest, f"aback_{s}")
            d_qkv.append(grads)
            parts = contract([grads], ids, attn_w, 0, n, 512, f"da_{s}")
            (low,) = back_step(
                x[s], line.scatter(parts, f"ra{s}"), gain_a, g_mid[s], f"fin_{s}", False
            )
            d_x.append(low)
        grad_out = weight_grad(flat_b, [att], "wgo")
        grad_qkv = weight_grad(flat_a, [[d[i] for d in d_qkv] for i in range(3)], "wgq")

        gain_sum = jnp.stack(
            [
                jnp.sum(attn_own[:, : 3 * heads_width].astype(F32) * grad_qkv, axis=1)
                / norm_attn[0].astype(F32),
                jnp.sum(mlp_own.astype(F32) * grad_gu, axis=1) / norm_mlp[0].astype(F32),
            ]
        )
        gain_sum = line.total(gain_sum, "gains")
        return (
            leave(outs, targets, "leave_o"),
            leave(d_x, targets, "leave_x"),
            grad_qkv[None, :, :heads_width],
            grad_qkv[None, :, heads_width : 2 * heads_width],
            grad_qkv[None, :, 2 * heads_width :],
            grad_out.T[None],
            grad_gu[None, :, :units],
            grad_gu[None, :, units:],
            grad_down.T[None],
            gain_sum[:1],
            gain_sum[1:],
        )

    return per_device


def solution(mesh):
    placed = (
        P("tensor", "dp", None),
        P("dp", None),
        P(None, "dp", "tensor"),
        P(None, "dp", "tensor"),
        P(None, "dp", "tensor"),
        P(None, "tensor", "dp"),
        P(None, "dp", "tensor"),
        P(None, "dp", "tensor"),
        P(None, "tensor", "dp"),
        P(None, "dp"),
        P(None, "dp"),
        P("tensor", "dp", None),
    )
    return jax.shard_map(
        build(mesh),
        mesh=mesh,
        in_specs=placed,
        out_specs=(
            P("tensor", "dp", None),
            P("tensor", "dp", None),
            P(None, "dp", "tensor"),
            P(None, "dp", "tensor"),
            P(None, "dp", "tensor"),
            P(None, "tensor", "dp"),
            P(None, "dp", "tensor"),
            P(None, "dp", "tensor"),
            P(None, "tensor", "dp"),
            P(None, "dp"),
            P(None, "dp"),
        ),
        check_vma=False,
    )
```
